32 devices in a mesh: atom: 16 (over z, x, core), energy: 2 (over y).
Axes of the slice: x: 2, y: 2, z: 4, core: 2. Of those that a mesh axis runs over, the one named last changes fastest.
Arguments:
- single_site: float32 [256, 2, 2, 1024], P('atom', 'energy'), may hold values from -2 to 2
- structure: float32 [2, 26, 2, 1024], P('energy'), may hold values from -0.4375 to 0.4375
- neighbours: int32 [256, 26], P('atom'), may hold values from 0 to 255, as said below
- species: int32 [256], P('atom'), may hold values from 0 to 1
- valence: float32 [2], replicated, may hold values from 0.5 to 3
- energy_weights: float32 [2, 2], P('energy'), may hold values from -4 to 4
- gaunt_table: float32 [49, 1024], replicated, may hold values from -1.5 to 1.5
- radial_shapes: float32 [2, 2, 2, 49, 512], P(None, 'energy'), may hold values from -6 to 6
- radial_weights: float32 [512], replicated, may hold values from 0.001 to 0.03
- madelung: float32 [256, 256], P('atom'), may hold values from -0.375 to 0.375
- old_potential: float32 [256, 49, 512], P('atom', None, 'energy'), may hold values from -6 to 6
Outputs:
- density: float32 [256, 49, 512], P('atom', None, 'energy')
- potential: float32 [256, 49, 512], P('atom', None, 'energy')
The draws below stay inside these ranges and needn't reach their ends.
Inputs may be any that keep to these rules, and one draw needn't show every extreme that they name: `neighbours`: atom a lies in lattice plane a // 16; the 16 planes close periodically. Slots 0 to 8 name distinct atoms of the plane before a's, slots 9 to 16 distinct atoms of a's own plane other than a, slots 17 to 25 distinct atoms of the plane after. Direction 26 - 1 - k is the reverse of direction k; this only says which structure constants pair up, and the neighbour lists need not be reciprocal.
All inputs are finite; a program needn't handle non-finite values.
Results may differ from the reference program's by a relative error of at most 0.0001.
Values sent between devices are 32-bit elements; how exact they have to be, the bound alone decides.
A program may use at most 64 MiB of HBM per device.

```python
import math
import jax
import jax.numpy as jnp
from jax import lax

ORDER = 32
DIRS = 26
LM = 49
RADIAL = 512
PLANE = 16
TERMS = 4
SPECIES = 2
ATOMS = 256
ENERGIES = 2


def draw_neighbours(key, part):
    plane_count = ATOMS // PLANE
    atom_ids = jnp.arange(ATOMS, dtype=jnp.int32)
    plane_index = atom_ids // PLANE
    position = atom_ids % PLANE
    slots = jnp.arange(PLANE, dtype=jnp.int32)[None, :]
    columns = []
    for offset, picked, stream in ((-1, 9, 11), (0, 8, 12), (1, 9, 13)):
        scores = jax.random.randint(jax.random.fold_in(key, stream), (ATOMS, PLANE), 0, 1 << 20, dtype=jnp.int32) * PLANE + slots
        if offset == 0:
            scores = jnp.where(slots == position[:, None], jnp.int32(1 << 30), scores)
        ranking = jnp.argsort(scores, axis=1)[:, :picked].astype(jnp.int32)
        target = ((plane_index + offset) % plane_count)[:, None] * PLANE + ranking
        columns.append(target)
    return jnp.concatenate(columns, axis=1).astype(jnp.int32)


def plant(values, own_key, smallest, largest):
    place = [jax.random.randint(jax.random.fold_in(own_key, axis), (), 0, length) for axis, length in enumerate(values.shape)]
    widest = values.shape.index(max(values.shape))
    beside = place[:widest] + [(place[widest] + 1) % values.shape[widest]] + place[widest + 1:]
    return values.at[tuple(place)].set(smallest).at[tuple(beside)].set(largest)


def shard_levels(key, shape, split, smallest, high):
    level, own = 1.0, jax.random.fold_in(key, 6)
    for dim, shards_of in split:
        heights = jnp.exp(jax.random.uniform(jax.random.fold_in(own, dim), (shards_of,), jnp.float32, smallest / len(split), high / len(split)))
        level = level * jnp.repeat(heights, shape[dim] // shards_of).reshape([-1 if axis == dim else 1 for axis in range(len(shape))])
    return level


def centred(own_key, extent, width, bound, cuts=(), kind=jnp.bfloat16):
    values = width * jax.random.normal(own_key, extent, jnp.float32)
    if cuts:
        values = values * shard_levels(own_key, extent, cuts, -0.22, 0.18)
    return jnp.clip(values, -bound, bound).astype(kind)


def setup_inputs(seed: int = 0) -> dict:
    key_list = jax.random.split(jax.random.key(seed), 12)
    return {
        "single_site": centred(key_list[0], (ATOMS, ENERGIES, 2, ORDER * ORDER), 0.125, 2.0, ((0, 16), (1, 2)), jnp.float32),
        "structure": centred(key_list[1], (ENERGIES, DIRS, 2, ORDER * ORDER), 0.03, 0.4375, ((0, 2),), jnp.float32),
        "neighbours": draw_neighbours(jax.random.fold_in(key_list[11], 71), 0),
        "species": plant(jax.random.randint(key_list[3], (ATOMS,), 0, SPECIES), jax.random.fold_in(key_list[3], 1), 0, SPECIES - 1).astype(jnp.int32),
        "valence": jnp.clip(jax.random.uniform(key_list[4], (SPECIES,), jnp.float32, 0.5, 3.0), 0.5, 3.0),
        "energy_weights": centred(key_list[5], (ENERGIES, 2), 1.0, 4.0, ((0, 2),), jnp.float32),
        "gaunt_table": centred(key_list[6], (LM, ORDER * ORDER), 16 ** -0.5, 1.5, (), jnp.float32),
        "radial_shapes": centred(key_list[7], (SPECIES, ENERGIES, 2, LM, RADIAL), 1.0, 6.0, ((1, 2),), jnp.float32),
        "radial_weights": jnp.clip(jnp.exp(jax.random.uniform(key_list[8], (RADIAL,), jnp.float32, math.log(0.001), math.log(0.03))), 0.001, 0.03),
        "madelung": centred(key_list[9], (ATOMS, ATOMS), ATOMS ** -0.5, 0.375, ((0, 16),), jnp.float32),
        "old_potential": centred(key_list[10], (ATOMS, LM, RADIAL), 1.0, 6.0, ((0, 16), (2, 2)), jnp.float32),
    }


mixing = 0.3
highest = lax.Precision.HIGHEST


def matmul_high(former, latter):
    return jnp.matmul(former, latter, precision=highest)


def complex_product(former, latter):
    former_real = former[..., 0, :, :]
    former_imag = former[..., 1, :, :]
    latter_real = latter[..., 0, :, :]
    latter_imag = latter[..., 1, :, :]
    real_part = matmul_high(former_real, latter_real) - matmul_high(former_imag, latter_imag)
    imag_part = matmul_high(former_real, latter_imag) + matmul_high(former_imag, latter_real)
    return jnp.stack([real_part, imag_part], axis=-3)


def reference(single_site, structure, neighbours, species, valence, energy_weights, gaunt_table, radial_shapes, radial_weights, madelung, old_potential):
    site_matrices = single_site.reshape(ATOMS, ENERGIES, 2, ORDER, ORDER)
    couplings = structure.reshape(ENERGIES, DIRS, 2, ORDER, ORDER)

    def add_direction(accumulated, direction):
        forward = lax.dynamic_index_in_dim(couplings, direction, 1, keepdims=False)
        backward = lax.dynamic_index_in_dim(couplings, DIRS - 1 - direction, 1, keepdims=False)
        column = lax.dynamic_index_in_dim(neighbours, direction, 1, keepdims=False)
        gathered = jnp.take(site_matrices, column, axis=0)
        return accumulated + complex_product(complex_product(forward, gathered), backward), None

    coupled, _ = lax.scan(add_direction, jnp.zeros_like(site_matrices), jnp.arange(DIRS, dtype=jnp.int32))
    propagator = complex_product(site_matrices, coupled)
    series_term = site_matrices
    path_operator = site_matrices
    for power in range(TERMS - 1):
        series_term = complex_product(propagator, series_term)
        path_operator = path_operator + series_term
    flat = path_operator.reshape(ATOMS, ENERGIES, 2, ORDER * ORDER)
    projected = jnp.einsum('aezq,lq->aezl', flat, gaunt_table, precision=highest)
    weight_real = energy_weights[:, 0][None, :, None]
    weight_imag = energy_weights[:, 1][None, :, None]
    scaled_real = weight_real * projected[:, :, 0] - weight_imag * projected[:, :, 1]
    scaled_imag = weight_real * projected[:, :, 1] + weight_imag * projected[:, :, 0]
    kinds = jnp.arange(SPECIES, dtype=jnp.int32)
    one_hot = jnp.where(species[:, None] == kinds[None, :], jnp.float32(1.0), jnp.float32(0.0))
    sorted_real = one_hot[:, :, None, None] * scaled_real[:, None]
    sorted_imag = one_hot[:, :, None, None] * scaled_imag[:, None]
    density = jnp.einsum('asel,selr->alr', sorted_real, radial_shapes[:, :, 1], precision=highest)
    density = density + jnp.einsum('asel,selr->alr', sorted_imag, radial_shapes[:, :, 0], precision=highest)
    valence_of = jnp.sum(one_hot * valence[None, :], axis=1)
    charges = jnp.dot(density[:, 0, :], radial_weights, precision=highest) - valence_of
    madelung_shift = jnp.dot(madelung, charges, precision=highest)
    channel = jnp.arange(LM, dtype=jnp.int32)[None, :, None]
    added = jnp.where(channel == 0, madelung_shift[:, None, None], jnp.float32(0.0))
    potential = (1.0 - mixing) * old_potential + mixing * (density + added)
    return density, potential
```

```python
import functools

import jax
import jax.numpy as jnp
from jax import lax
from jax.experimental import pallas as pl
from jax.experimental.pallas import tpu as pltpu
from jax.sharding import PartitionSpec as P

PLANE = 16
TERMS = 4
LANES = 128

mixing = 0.3
f32 = jnp.float32
bf16 = jnp.bfloat16


def split(x):
    high = x.astype(bf16)
    return high, (x - high.astype(f32)).astype(bf16)


def tile_masks(rows):
    lane = lax.broadcasted_iota(jnp.int32, (rows, LANES), 1)
    return lane < 64, (lane & 32) == 0


def times_i(x, real_lane):
    return jnp.where(real_lane, -pltpu.roll(x, 96, 1), pltpu.roll(x, 32, 1))


def dot(a, b):
    return jnp.dot(a, b, preferred_element_type=f32)


def prepare_couplings(g_ref, rhs_ref, order, blocks):
    _, real_lane = tile_masks(order)
    for t in range(blocks):
        lanes = pl.ds(t * LANES, LANES)
        g = g_ref[:, lanes]
        high, low = split(jnp.concatenate([g, times_i(g, real_lane)], axis=0))
        rhs_ref[:, lanes] = jnp.concatenate([high, high, low, low], axis=0)


def plane_products(x, lhs_ref, rhs_ref, rhigh_ref, rlow_ref, plane, first, count, order):
    low_lane, _ = tile_masks(order)
    for pair in range(PLANE // 2):
        v = x(pair)
        high = v.astype(bf16).astype(f32)
        low = v - high
        even = jnp.where(low_lane, high, pltpu.roll(low, 64, 1))
        odd = jnp.where(low_lane, pltpu.roll(high, 64, 1), low)
        lhs_ref[pl.ds(pair * 2 * order, 2 * order), :] = jnp.concatenate(
            [even, odd], axis=0
        ).astype(bf16)
    lhs = lhs_ref[...]
    lhs = jnp.concatenate([lhs, lhs], axis=1)
    for t in range(count):
        r = dot(lhs, rhs_ref[:, pl.ds((first + t) * LANES, LANES)])
        high, low = split(r)
        rhigh_ref[plane, t] = high
        rlow_ref[plane, t] = low


def gather(nbr_ref, rhigh_ref, rlow_ref, yhigh_ref, ylow_ref, dirs, firsts, order):
    for b in range(dirs):
        k = dirs - 1 - b
        plane = 0 if k < 9 else (1 if k < 17 else 2)
        t = b // 2
        half = pl.ds((b % 2) * 64, 64)
        for a in range(PLANE):
            n = nbr_ref[a, k]
            rows = pl.ds(pl.multiple_of(n * order, order), order)
            to = (pl.ds(t * order, order), pl.ds(a * LANES + (b % 2) * 64, 64))
            yhigh_ref[to] = rhigh_ref[plane, t - firsts[plane], rows, half]
            ylow_ref[to] = rlow_ref[plane, t - firsts[plane], rows, half]


def block_diagonal(v, low_lane, real_lane):
    turned = times_i(v, real_lane)
    zero = jnp.zeros_like(v)
    return jnp.concatenate(
        [
            jnp.where(low_lane, v, zero),
            jnp.where(low_lane, turned, zero),
            jnp.where(low_lane, zero, v),
            jnp.where(low_lane, zero, turned),
        ],
        axis=0,
    )


def weights_of(v, low_lane, real_lane):
    high, low = split(block_diagonal(v, low_lane, real_lane))
    return jnp.concatenate([high, low], axis=1)


def pair_product(u, weights, order):
    high, low = split(u)
    o = dot(jnp.concatenate([high, low], axis=0), weights)
    return o[:order, :LANES] + o[order:, :LANES] + o[:order, LANES:]


def path_and_project(own, g2_ref, yhigh_ref, ylow_ref, gaunt_ref, v_ref, order):
    low_lane, real_lane = tile_masks(order)
    low2, _ = tile_masks(2 * order)
    gh, gl = split(g2_ref[...])
    rows = gh.shape[0]
    both = jnp.concatenate([gh, gl], axis=0)
    for pair in range(PLANE // 2):
        lanes = pl.ds(pair * 2 * LANES, 2 * LANES)
        d = dot(both, yhigh_ref[:, lanes])
        s = d[:rows] + d[rows:] + dot(gh, ylow_ref[:, lanes])
        half = rows // 2
        e0, o0 = s[:half, :LANES], s[half:, :LANES]
        e1, o1 = s[:half, LANES:], s[half:, LANES:]
        m = jnp.where(low2, e0, o1) + pltpu.roll(jnp.where(low2, e1, o0), 64, 1)
        c = m[:order] + times_i(m[order:], real_lane)
        t = own(pair)
        q = pair_product(c, weights_of(t, low_lane, real_lane), order)
        wq = weights_of(q, low_lane, real_lane)
        v = t
        for _ in range(TERMS - 1):
            v = t + pair_product(v, wq, order)
        v_ref[pl.ds(pair * order, order), :] = v
    pairs = PLANE // 2
    lane = lax.broadcasted_iota(jnp.int32, (pairs, LANES), 1) // 32
    columns = []
    for block in range(order // 4):
        us = [v_ref[pl.ds(4 * block + ii, pairs, stride=order), :] for ii in range(4)]
        pieces = []
        for part in range(4):
            z = us[0] if part == 0 else pltpu.roll(us[0], (-part * 32) % LANES, 1)
            for ii in range(1, 4):
                shift = ((ii - part) * 32) % LANES
                z = jnp.where(lane == ii, us[ii] if shift == 0 else pltpu.roll(us[ii], shift, 1), z)
            pieces.append(z)
        columns.append(jnp.concatenate(pieces, axis=0))
    z = jnp.concatenate(columns, axis=1)
    zh, zl = split(z)
    gh, gl = split(gaunt_ref[...])
    nt = (((1,), (1,)), ((), ()))
    d = lax.dot_general(jnp.concatenate([zh, zl], axis=0), gh, nt, preferred_element_type=f32)
    return d[: 2 * PLANE] + d[2 * PLANE :] + lax.dot_general(zh, gl, nt, preferred_element_type=f32)


def store_scaled(projected, wr, wi, coef_ref):
    pairs = PLANE // 2
    for a2 in range(2):
        re = projected[a2 * 2 * pairs : a2 * 2 * pairs + pairs]
        im = projected[a2 * 2 * pairs + pairs : (a2 + 1) * 2 * pairs]
        coef_ref[0, pl.ds(a2, pairs, stride=2), :] = wr * re - wi * im
        coef_ref[1, pl.ds(a2, pairs, stride=2), :] = wr * im + wi * re


def plan(dirs):
    ends = ((0, 9), (9, 17), (17, dirs))
    firsts = tuple((dirs - stop) // 2 for _, stop in ends)
    counts = tuple((dirs - 1 - start) // 2 - first + 1 for (start, _), first in zip(ends, firsts))
    return firsts, counts


def core(order, dirs, nbr_ref, w_ref, low_ref, own_ref, high_ref, g_ref, g2_ref, gaunt_ref,
         coef_ref, rhs_ref, lhs_ref, rhigh_ref, rlow_ref, yhigh_ref, ylow_ref, v_ref):
    firsts, counts = plan(dirs)
    prepare_couplings(g_ref, rhs_ref, order, dirs // 2)
    for plane, ref in ((1, own_ref), (0, low_ref), (2, high_ref)):
        x = lambda pair, ref=ref: ref[:, pl.ds(pair * LANES, LANES)]
        plane_products(x, lhs_ref, rhs_ref, rhigh_ref, rlow_ref, plane, firsts[plane], counts[plane], order)
    gather(nbr_ref, rhigh_ref, rlow_ref, yhigh_ref, ylow_ref, dirs, firsts, order)
    own = lambda pair: own_ref[:, pl.ds(pair * LANES, LANES)]
    projected = path_and_project(own, g2_ref, yhigh_ref, ylow_ref, gaunt_ref, v_ref, order)
    store_scaled(projected, w_ref[0, 0], w_ref[0, 1], coef_ref)


def core_scratch(order, dirs):
    count = max(plan(dirs)[1])
    depth = dirs // 2 * order
    return [
        pltpu.VMEM((8 * order, dirs * 64), bf16),
        pltpu.VMEM((PLANE * order, LANES), bf16),
        pltpu.VMEM((3, count, PLANE * order, LANES), bf16),
        pltpu.VMEM((3, count, PLANE * order, LANES), bf16),
        pltpu.VMEM((depth, PLANE * LANES), bf16),
        pltpu.VMEM((depth, PLANE * LANES), bf16),
        pltpu.VMEM((PLANE // 2 * order, LANES), f32),
    ]


def density_kernel(species_ref, coef_ref, pieces_ref, shift_ref, old_ref, density_ref, potential_ref):
    kinds, energies = pieces_ref.shape[0], pieces_ref.shape[1]
    channels, atoms, width = density_ref.shape
    kind = jnp.broadcast_to(species_ref[...], (atoms, width))
    for l in range(channels):
        total = None
        for e in range(energies):
            for z in range(2):
                row = jnp.broadcast_to(pieces_ref[0, e, 1 - z, l : l + 1, :], (atoms, width))
                for s in range(1, kinds):
                    row = jnp.where(kind == s, pieces_ref[s, e, 1 - z, l : l + 1, :], row)
                term = coef_ref[e, z, :, l : l + 1] * row
                total = term if total is None else total + term
        density_ref[l] = total
        added = total + shift_ref[...] if l == 0 else total
        potential_ref[l] = (1.0 - mixing) * old_ref[l] + mixing * added


VMEM = pl.BlockSpec(memory_space=pltpu.VMEM)
SMEM = pl.BlockSpec(memory_space=pltpu.SMEM)


def neighbour_rings(count):
    forward = [(i, (i + 1) % count) for i in range(count)]
    return forward, [(target, source) for source, target in forward]


def shards(single_site, structure, neighbours, species, valence, energy_weights, gaunt_table,
           radial_shapes, radial_weights, madelung, old_potential):
    atom_rows, energy_rows = single_site.shape[:2]
    dirs = structure.shape[1]
    order = int(round(single_site.shape[3] ** 0.5))
    channels, width = old_potential.shape[1], old_potential.shape[2]
    kinds = radial_shapes.shape[0]
    energies = lax.axis_size("energy")
    assert atom_rows == PLANE and energy_rows == 1 and order == 32

    own = single_site.reshape(atom_rows, 2, order, order)
    own = jnp.transpose(own, (2, 0, 1, 3)).reshape(order, atom_rows * 2 * order)
    forward, backward = neighbour_rings(lax.axis_size("atom"))
    low = lax.ppermute(own, "atom", forward)
    high = lax.ppermute(own, "atom", backward)
    pieces = lax.all_to_all(radial_shapes, "energy", split_axis=4, concat_axis=1, tiled=True)

    g = structure.reshape(dirs, 2, order, order)
    g_rows = jnp.transpose(g, (2, 0, 1, 3)).reshape(order, dirs * 2 * order)
    g2 = g[::-1].reshape(dirs // 2, 2, 2, order, order)
    g2 = jnp.transpose(g2, (1, 2, 3, 0, 4)).reshape(4 * order, dirs // 2 * order)

    coef = pl.pallas_call(
        functools.partial(core, order, dirs),
        out_shape=jax.ShapeDtypeStruct((2, atom_rows, channels), f32),
        in_specs=[SMEM, SMEM] + [VMEM] * 6,
        out_specs=VMEM,
        scratch_shapes=core_scratch(order, dirs),
        name="scatter",
    )(neighbours % PLANE, energy_weights, low, own, high, g_rows, g2, gaunt_table)

    shape_charge = jnp.sum(radial_shapes[:, 0, :, 0, :] * radial_weights, axis=-1)
    sums = shape_charge[species]
    part = coef[0, :, 0] * sums[:, 1] + coef[1, :, 0] * sums[:, 0]
    local = lax.psum(part, "energy") - valence[species]
    charges = lax.all_gather(local, "atom", axis=0, tiled=True)
    shift = jnp.sum(madelung * charges[None, :], axis=1, keepdims=True)
    coef_all = lax.all_gather(coef, "energy", axis=0)

    old = jnp.transpose(old_potential, (1, 0, 2))
    density, potential = pl.pallas_call(
        density_kernel,
        out_shape=[jax.ShapeDtypeStruct(old.shape, f32)] * 2,
        in_specs=[VMEM] * 5,
        out_specs=[VMEM] * 2,
        name="density",
    )(species[:, None], coef_all, pieces, shift, old)
    back = lambda x: jnp.transpose(x, (1, 0, 2))
    return back(density), back(potential)


def solution(mesh):
    in_specs = (
        P("atom", "energy", None, None),
        P("energy", None, None, None),
        P("atom", None),
        P("atom"),
        P(),
        P("energy", None),
        P(),
        P(None, "energy", None, None, None),
        P(),
        P("atom", None),
        P("atom", None, "energy"),
    )
    out_specs = (P("atom", None, "energy"), P("atom", None, "energy"))
    return jax.shard_map(shards, mesh=mesh, in_specs=in_specs, out_specs=out_specs, check_vma=False)
```

```python
import functools

import jax
import jax.numpy as jnp
from jax import lax
from jax.experimental import pallas as pl
from jax.experimental.pallas import tpu as pltpu
from jax.sharding import PartitionSpec as P

PLANE = 16
TERMS = 4
LANES = 128

mixing = 0.3
f32 = jnp.float32
bf16 = jnp.bfloat16


def split(x):
    high = x.astype(bf16)
    return high, (x - high.astype(f32)).astype(bf16)


def tile_masks(rows):
    lane = lax.broadcasted_iota(jnp.int32, (rows, LANES), 1)
    return lane < 64, (lane & 32) == 0


def times_i(x, real_lane):
    return jnp.where(real_lane, -pltpu.roll(x, 96, 1), pltpu.roll(x, 32, 1))


def dot(a, b):
    return jnp.dot(a, b, preferred_element_type=f32)


def to_rows(raw, tiles, w_ref, order):
    stride = w_ref.shape[0] // order
    lane = lax.broadcasted_iota(jnp.int32, (tiles, LANES), 1) // 32
    for block in range(order // 4):
        parts = [raw(m, pl.ds(block * LANES, LANES)) for m in range(4)]
        for ii in range(4):
            u = None
            for m in range(4):
                shift = ((m - ii) * 32) % LANES
                x = parts[m] if shift == 0 else pltpu.roll(parts[m], shift, 1)
                u = x if u is None else jnp.where(lane == m, x, u)
            w_ref[pl.ds((4 * block + ii) * stride, tiles), :] = u


def tile_of(w_ref, tile, order):
    return w_ref[pl.ds(tile, order, stride=w_ref.shape[0] // order), :]


def prepare_couplings(w_ref, rhs_ref, g2_ref, order, blocks):
    _, real_lane = tile_masks(order)
    lane = lax.broadcasted_iota(jnp.int32, (order, LANES), 1) // 32
    joined = [None] * 4
    for t in range(blocks):
        g = tile_of(w_ref, t, order)
        high, low = split(jnp.concatenate([g, times_i(g, real_lane)], axis=0))
        rhs_ref[:, pl.ds(t * LANES, LANES)] = jnp.concatenate([high, high, low, low], axis=0)
    for t in range(blocks):
        g = tile_of(w_ref, blocks - 1 - t, order)
        place = t % 4
        for parity in range(2):
            for z in range(2):
                row = parity * 2 + z
                chunk = (2 - 2 * parity + z) % 4
                shift = ((place - chunk) * 32) % LANES
                x = g if shift == 0 else pltpu.roll(g, shift, 1)
                joined[row] = x if place == 0 else jnp.where(lane == place, x, joined[row])
                if place == 3 or t == blocks - 1:
                    g2_ref[pl.ds(row * order, order), pl.ds(t // 4 * LANES, 32 * (place + 1))] = (
                        joined[row][:, : 32 * (place + 1)]
                    )


def plane_products(x, lhs_ref, rhs_ref, rhigh_ref, rlow_ref, plane, first, count, order):
    low_lane, _ = tile_masks(order)
    for pair in range(PLANE // 2):
        v = x(pair)
        high = v.astype(bf16).astype(f32)
        low = v - high
        even = jnp.where(low_lane, high, pltpu.roll(low, 64, 1))
        odd = jnp.where(low_lane, pltpu.roll(high, 64, 1), low)
        lhs_ref[pl.ds(pair * 2 * order, 2 * order), :] = jnp.concatenate(
            [even, odd], axis=0
        ).astype(bf16)
    lhs = lhs_ref[...]
    lhs = jnp.concatenate([lhs, lhs], axis=1)
    for t in range(count):
        r = dot(lhs, rhs_ref[:, pl.ds((first + t) * LANES, LANES)])
        high, low = split(r)
        rhigh_ref[plane, t] = high.reshape(PLANE, order, LANES)
        rlow_ref[plane, t] = low.reshape(PLANE, order, LANES)


def gather(nbr_ref, rhigh_ref, rlow_ref, yhigh_ref, ylow_ref, dirs, plane, first, order):
    start, stop = ends_of(dirs)[plane]
    for k in range(start, stop):
        b = dirs - 1 - k
        t = b // 2
        half = slice((b % 2) * 64, (b % 2) * 64 + 64)
        for a in range(PLANE):
            n = nbr_ref[a, k]
            to = (pl.ds(t * order, order), pl.ds(a * LANES + (b % 2) * 64, 64))
            yhigh_ref[to] = rhigh_ref[plane, t - first, n][:, half]
            ylow_ref[to] = rlow_ref[plane, t - first, n][:, half]


def block_diagonal(v, low_lane, real_lane):
    turned = times_i(v, real_lane)
    zero = jnp.zeros_like(v)
    return jnp.concatenate(
        [
            jnp.where(low_lane, v, zero),
            jnp.where(low_lane, turned, zero),
            jnp.where(low_lane, zero, v),
            jnp.where(low_lane, zero, turned),
        ],
        axis=0,
    )


def weights_of(v, low_lane, real_lane):
    high, low = split(block_diagonal(v, low_lane, real_lane))
    return jnp.concatenate([high, low], axis=1)


def pair_product(u, weights, order):
    high, low = split(u)
    o = dot(jnp.concatenate([high, low], axis=0), weights)
    return o[:order, :LANES] + o[order:, :LANES] + o[:order, LANES:]


def path_and_project(own, g2_ref, yhigh_ref, ylow_ref, gaunt_ref, v_ref, order):
    low_lane, real_lane = tile_masks(order)
    low2, _ = tile_masks(2 * order)
    gh, gl = split(g2_ref[...])
    rows = gh.shape[0]
    both = jnp.concatenate([gh, gl], axis=0)
    for pair in range(PLANE // 2):
        lanes = pl.ds(pair * 2 * LANES, 2 * LANES)
        d = dot(both, yhigh_ref[:, lanes])
        s = d[:rows] + d[rows:] + dot(gh, ylow_ref[:, lanes])
        half = rows // 2
        e0, o0 = s[:half, :LANES], s[half:, :LANES]
        e1, o1 = s[:half, LANES:], s[half:, LANES:]
        m = jnp.where(low2, e0, o1) + pltpu.roll(jnp.where(low2, e1, o0), 64, 1)
        c = m[:order] + times_i(m[order:], real_lane)
        t = own(pair)
        q = pair_product(c, weights_of(t, low_lane, real_lane), order)
        wq = weights_of(q, low_lane, real_lane)
        v = t
        for _ in range(TERMS - 1):
            v = t + pair_product(v, wq, order)
        v_ref[pl.ds(pair * order, order), :] = v
    pairs = PLANE // 2
    lane = lax.broadcasted_iota(jnp.int32, (pairs, LANES), 1) // 32
    columns = []
    for block in range(order // 4):
        us = [v_ref[pl.ds(4 * block + ii, pairs, stride=order), :] for ii in range(4)]
        pieces = []
        for part in range(4):
            z = us[0] if part == 0 else pltpu.roll(us[0], (-part * 32) % LANES, 1)
            for ii in range(1, 4):
                shift = ((ii - part) * 32) % LANES
                z = jnp.where(lane == ii, us[ii] if shift == 0 else pltpu.roll(us[ii], shift, 1), z)
            pieces.append(z)
        columns.append(jnp.concatenate(pieces, axis=0))
    z = jnp.concatenate(columns, axis=1)
    zh, zl = split(z)
    gh, gl = split(gaunt_ref[...])
    nt = (((1,), (1,)), ((), ()))
    d = lax.dot_general(jnp.concatenate([zh, zl], axis=0), gh, nt, preferred_element_type=f32)
    return d[: 2 * PLANE] + d[2 * PLANE :] + lax.dot_general(zh, gl, nt, preferred_element_type=f32)


def store_scaled(projected, wr, wi, coef_ref):
    pairs = PLANE // 2
    for a2 in range(2):
        re = projected[a2 * 2 * pairs : a2 * 2 * pairs + pairs]
        im = projected[a2 * 2 * pairs + pairs : (a2 + 1) * 2 * pairs]
        coef_ref[0, pl.ds(a2, pairs, stride=2), :] = wr * re - wi * im
        coef_ref[1, pl.ds(a2, pairs, stride=2), :] = wr * im + wi * re


def ends_of(dirs):
    return ((0, 9), (9, 17), (17, dirs))


def plan(dirs):
    ends = ends_of(dirs)
    firsts = tuple((dirs - stop) // 2 for _, stop in ends)
    counts = tuple((dirs - 1 - start) // 2 - first + 1 for (start, _), first in zip(ends, firsts))
    return firsts, counts


def core(order, dirs, ring, energies, nbr_ref, w_ref, valence_ref, own_ref, g_ref, gaunt_ref, shapes_ref,
         weights_ref, species_ref, madelung_ref, coef_ref, pieces_ref, shift_ref,
         halo_ref, q_ref, mine_ref, wg_ref, wt_ref, rhs_ref, g2_ref, lhs_ref, rhigh_ref, rlow_ref,
         yhigh_ref, ylow_ref, v_ref, halo_send, halo_recv, piece_send, piece_recv, coef_send, coef_recv,
         q_send, q_recv, local_sem):
    atom, energy = lax.axis_index("atom"), lax.axis_index("energy")
    devices = ring * energies
    me = atom * energies + energy
    kinds, width = shapes_ref.shape[0], pieces_ref.shape[4]

    def place(step):
        other = lax.rem(me + step, devices)
        return {"atom": other // energies, "energy": lax.rem(other, energies)}

    barrier = pltpu.get_barrier_semaphore()

    def greet(step, carry):
        pl.semaphore_signal(barrier, inc=1, device_id=place(step), device_id_type=MESH)
        return carry

    lax.fori_loop(1, devices, greet, 0)

    firsts, counts = plan(dirs)
    to_rows(lambda m, lanes: g_ref[m, :, lanes], dirs // 2, wg_ref, order)
    prepare_couplings(wg_ref, rhs_ref, g2_ref, order, dirs // 2)
    pl.semaphore_wait(barrier, devices - 1)

    right, left = lax.rem(atom + 1, ring), lax.rem(atom + ring - 1, ring)
    halos = []
    for side, target in ((0, right), (1, left)):
        copy = pltpu.make_async_remote_copy(
            src_ref=own_ref, dst_ref=halo_ref.at[side], send_sem=halo_send.at[side],
            recv_sem=halo_recv.at[side], device_id={"atom": target, "energy": energy}, device_id_type=MESH,
        )
        copy.start()
        halos.append(copy)

    def slice_of(e):
        return shapes_ref.at[:, :, :, pl.ds(pl.multiple_of(e * width, LANES), width)]

    pieces = []
    for step in range(1, energies):
        other = lax.rem(energy + step, energies)
        copy = pltpu.make_async_remote_copy(
            src_ref=slice_of(other), dst_ref=pieces_ref.at[energy], send_sem=piece_send.at[step],
            recv_sem=piece_recv.at[step], device_id={"atom": atom, "energy": other}, device_id_type=MESH,
        )
        copy.start()
        pieces.append(copy)
    keep = pltpu.make_async_copy(slice_of(energy), pieces_ref.at[energy], local_sem)
    keep.start()

    def plane(index, raw):
        w = wt_ref.at[index]
        to_rows(raw, PLANE // 2, w, order)
        plane_products(lambda pair: tile_of(w, pair, order), lhs_ref, rhs_ref, rhigh_ref, rlow_ref,
                       index, firsts[index], counts[index], order)
        gather(nbr_ref, rhigh_ref, rlow_ref, yhigh_ref, ylow_ref, dirs, index, firsts[index], order)

    plane(1, lambda m, lanes: own_ref[m, :, lanes])

    kind = species_ref[...]
    sums = [None, None]
    base = jnp.zeros(kind.shape, f32)
    for s in range(kinds):
        total = jnp.sum(shapes_ref[s, 0] * weights_ref[...], axis=1, keepdims=True)
        for z in range(2):
            value = jnp.broadcast_to(total[1 - z : 2 - z], kind.shape)
            sums[z] = value if s == 0 else jnp.where(kind == s, value, sums[z])
        base = jnp.where(kind == s, valence_ref[s], base)
    base = jnp.where(energy == 0, base, jnp.zeros_like(base))

    for side, index in ((0, 0), (1, 2)):
        halos[side].wait_recv()
        plane(index, lambda m, lanes, side=side: halo_ref[side, m, :, lanes])

    own = lambda pair: tile_of(wt_ref.at[1], pair, order)
    projected = path_and_project(own, g2_ref, yhigh_ref, ylow_ref, gaunt_ref, v_ref, order)
    store_scaled(projected, w_ref[0, 0], w_ref[0, 1], mine_ref)

    q = mine_ref[0, :, 0:1] * sums[0] + mine_ref[1, :, 0:1] * sums[1] - base
    row = lax.broadcasted_iota(jnp.int32, (PLANE, LANES), 0)
    lane = lax.broadcasted_iota(jnp.int32, (PLANE, LANES), 1)
    spot = lane == row + PLANE * lax.rem(atom, LANES // PLANE)
    q_ref[me] = jnp.sum(jnp.where(spot, q, jnp.zeros((PLANE, LANES), f32)), axis=0, keepdims=True)

    def spread(step, carry):
        pltpu.make_async_remote_copy(
            src_ref=q_ref.at[me], dst_ref=q_ref.at[me], send_sem=q_send, recv_sem=q_recv,
            device_id=place(step), device_id_type=MESH,
        ).start()
        return carry

    lax.fori_loop(1, devices, spread, 0)
    coefs = []
    for step in range(1, energies):
        other = lax.rem(energy + step, energies)
        copy = pltpu.make_async_remote_copy(
            src_ref=mine_ref, dst_ref=coef_ref.at[energy], send_sem=coef_send.at[step],
            recv_sem=coef_recv.at[step], device_id={"atom": atom, "energy": other}, device_id_type=MESH,
        )
        copy.start()
        coefs.append(copy)
    coef_ref[energy] = mine_ref[...]

    keep.wait()
    for copy in halos:
        copy.wait_send()
    for copy in pieces + coefs:
        copy.wait()
    rest = q_ref.at[pl.ds(0, devices - 1)]
    pltpu.make_async_copy(rest, rest, q_send).wait()
    pltpu.make_async_copy(rest, rest, q_recv).wait()
    group = LANES // PLANE * energies
    shift = jnp.zeros((PLANE, 1), f32)
    for g in range(ring * PLANE // LANES):
        charges = jnp.sum(q_ref[pl.ds(g * group, group), 0, :], axis=0, keepdims=True)
        shift = shift + jnp.sum(madelung_ref[:, pl.ds(g * LANES, LANES)] * charges, axis=1, keepdims=True)
    shift_ref[...] = shift


def core_scratch(order, dirs, ring, energies, channels):
    count = max(plan(dirs)[1])
    depth = dirs // 2 * order
    dma = pltpu.SemaphoreType.DMA
    return [
        pltpu.VMEM((2, 4, PLANE // 2, order * order), f32),
        pltpu.VMEM((ring * energies, 1, LANES), f32),
        pltpu.VMEM((2, PLANE, channels), f32),
        pltpu.VMEM((order * 16, LANES), f32),
        pltpu.VMEM((3, order * (PLANE // 2), LANES), f32),
        pltpu.VMEM((8 * order, dirs * 64), bf16),
        pltpu.VMEM((4 * order, depth), f32),
        pltpu.VMEM((PLANE * order, LANES), bf16),
        pltpu.VMEM((3, count, PLANE, order, LANES), bf16),
        pltpu.VMEM((3, count, PLANE, order, LANES), bf16),
        pltpu.VMEM((depth, PLANE * LANES), bf16),
        pltpu.VMEM((depth, PLANE * LANES), bf16),
        pltpu.VMEM((PLANE // 2 * order, LANES), f32),
        dma((2,)), dma((2,)), dma((energies,)), dma((energies,)), dma((energies,)), dma((energies,)),
        dma, dma, dma,
    ]


def density_kernel(species_ref, coef_ref, pieces_ref, shift_ref, old_ref, density_ref, potential_ref):
    kinds, energies = pieces_ref.shape[1], pieces_ref.shape[0]
    channels, atoms, width = density_ref.shape
    kind = jnp.broadcast_to(species_ref[...], (atoms, width))
    for l in range(channels):
        total = None
        for e in range(energies):
            for z in range(2):
                row = jnp.broadcast_to(pieces_ref[e, 0, l, 1 - z : 2 - z, :], (atoms, width))
                for s in range(1, kinds):
                    row = jnp.where(kind == s, pieces_ref[e, s, l, 1 - z : 2 - z, :], row)
                term = coef_ref[e, z, :, l : l + 1] * row
                total = term if total is None else total + term
        density_ref[l] = total
        added = total + shift_ref[...] if l == 0 else total
        potential_ref[l] = (1.0 - mixing) * old_ref[l] + mixing * added


VMEM = pl.BlockSpec(memory_space=pltpu.VMEM)
SMEM = pl.BlockSpec(memory_space=pltpu.SMEM)
MESH = pl.DeviceIdType.MESH


def shards(single_site, structure, neighbours, species, valence, energy_weights, gaunt_table,
           radial_shapes, radial_weights, madelung, old_potential):
    atom_rows, energy_rows = single_site.shape[:2]
    dirs = structure.shape[1]
    order = int(round(single_site.shape[3] ** 0.5))
    channels, width = old_potential.shape[1], old_potential.shape[2]
    kinds = radial_shapes.shape[0]
    energies = lax.axis_size("energy")
    assert atom_rows == PLANE and energy_rows == 1 and order == 32

    def parts(x):
        return jnp.transpose(x.reshape(-1, 4, order * order), (1, 0, 2))

    shapes = jnp.transpose(radial_shapes[:, 0], (0, 2, 1, 3))
    ring = lax.axis_size("atom")
    coef, pieces, shift = pl.pallas_call(
        functools.partial(core, order, dirs, ring, energies),
        out_shape=[
            jax.ShapeDtypeStruct((energies, 2, atom_rows, channels), f32),
            jax.ShapeDtypeStruct((energies, kinds, channels, 2, width), f32),
            jax.ShapeDtypeStruct((atom_rows, 1), f32),
        ],
        in_specs=[SMEM] * 3 + [VMEM] * 7,
        out_specs=[VMEM] * 3,
        scratch_shapes=core_scratch(order, dirs, ring, energies, channels),
        compiler_params=pltpu.CompilerParams(collective_id=0, has_side_effects=True),
        name="scatter",
    )(neighbours % PLANE, energy_weights, valence, parts(single_site), parts(structure), gaunt_table, shapes,
      radial_weights[None, :], species[:, None], madelung)

    old = jnp.transpose(old_potential, (1, 0, 2))
    density, potential = pl.pallas_call(
        density_kernel,
        out_shape=[jax.ShapeDtypeStruct(old.shape, f32)] * 2,
        in_specs=[VMEM] * 5,
        out_specs=[VMEM] * 2,
        name="density",
    )(species[:, None], coef, pieces, shift, old)
    back = lambda x: jnp.transpose(x, (1, 0, 2))
    return back(density), back(potential)


def solution(mesh):
    in_specs = (
        P("atom", "energy", None, None),
        P("energy", None, None, None),
        P("atom", None),
        P("atom"),
        P(),
        P("energy", None),
        P(),
        P(None, "energy", None, None, None),
        P(),
        P("atom", None),
        P("atom", None, "energy"),
    )
    out_specs = (P("atom", None, "energy"), P("atom", None, "energy"))
    return jax.shard_map(shards, mesh=mesh, in_specs=in_specs, out_specs=out_specs, check_vma=False)
```

```python
import functools

import jax
import jax.numpy as jnp
from jax import lax
from jax.experimental import pallas as pl
from jax.experimental.pallas import tpu as pltpu
from jax.sharding import PartitionSpec as P

PLANE = 16
TERMS = 4
LANES = 128

mixing = 0.3
f32 = jnp.float32
bf16 = jnp.bfloat16


def split(x):
    high = x.astype(bf16)
    return high, (x - high.astype(f32)).astype(bf16)


def tile_masks(rows):
    lane = lax.broadcasted_iota(jnp.int32, (rows, LANES), 1)
    return lane < 64, (lane & 32) == 0


def times_i(x, real_lane):
    return jnp.where(real_lane, -pltpu.roll(x, 96, 1), pltpu.roll(x, 32, 1))


def dot(a, b):
    return jnp.dot(a, b, preferred_element_type=f32)


def to_rows(raw, tiles, w_ref, order):
    stride = w_ref.shape[0] // order
    lane = lax.broadcasted_iota(jnp.int32, (tiles, LANES), 1) // 32
    for block in range(order // 4):
        parts = [raw(m, pl.ds(block * LANES, LANES)) for m in range(4)]
        for ii in range(4):
            u = None
            for m in range(4):
                shift = ((m - ii) * 32) % LANES
                x = parts[m] if shift == 0 else pltpu.roll(parts[m], shift, 1)
                u = x if u is None else jnp.where(lane == m, x, u)
            w_ref[pl.ds((4 * block + ii) * stride, tiles), :] = u


def tile_of(w_ref, tile, order):
    return w_ref[pl.ds(tile, order, stride=w_ref.shape[0] // order), :]


def prepare_couplings(w_ref, rhs_ref, g2_ref, order, blocks):
    _, real_lane = tile_masks(order)
    lane = lax.broadcasted_iota(jnp.int32, (order, LANES), 1) // 32
    joined = [None] * 4
    for t in range(blocks):
        g = tile_of(w_ref, t, order)
        high, low = split(jnp.concatenate([g, times_i(g, real_lane)], axis=0))
        rhs_ref[:, pl.ds(t * LANES, LANES)] = jnp.concatenate([high, high, low, low], axis=0)
    for t in range(blocks):
        g = tile_of(w_ref, blocks - 1 - t, order)
        place = t % 4
        for parity in range(2):
            for z in range(2):
                row = parity * 2 + z
                chunk = (2 - 2 * parity + z) % 4
                shift = ((place - chunk) * 32) % LANES
                x = g if shift == 0 else pltpu.roll(g, shift, 1)
                joined[row] = x if place == 0 else jnp.where(lane == place, x, joined[row])
                if place == 3 or t == blocks - 1:
                    lanes = pl.ds(t // 4 * LANES, 32 * (place + 1))
                    high, low = split(joined[row][:, : 32 * (place + 1)])
                    g2_ref[pl.ds(row * order, order), lanes] = high
                    g2_ref[pl.ds((4 + row) * order, order), lanes] = low


def plane_products(x, lhs_ref, rhs_ref, rhigh_ref, rlow_ref, plane, first, count, order):
    low_lane, _ = tile_masks(order)
    for pair in range(PLANE // 2):
        v = x(pair)
        high = v.astype(bf16).astype(f32)
        low = v - high
        even = jnp.where(low_lane, high, pltpu.roll(low, 64, 1))
        odd = jnp.where(low_lane, pltpu.roll(high, 64, 1), low)
        lhs_ref[pl.ds(pair * 2 * order, 2 * order), :] = jnp.concatenate(
            [even, odd], axis=0
        ).astype(bf16)
    lhs = lhs_ref[...]
    lhs = jnp.concatenate([lhs, lhs], axis=1)
    for t in range(count):
        r = dot(lhs, rhs_ref[:, pl.ds((first + t) * LANES, LANES)])
        high, low = split(r)
        rhigh_ref[plane, t] = high.reshape(PLANE, order, LANES)
        rlow_ref[plane, t] = low.reshape(PLANE, order, LANES)


def gather(nbr_ref, rhigh_ref, rlow_ref, yhigh_ref, ylow_ref, dirs, plane, first, order):
    start, stop = ends_of(dirs)[plane]
    for k in range(start, stop):
        b = dirs - 1 - k
        t = b // 2
        half = slice((b % 2) * 64, (b % 2) * 64 + 64)
        for a in range(PLANE):
            n = nbr_ref[a, k] & (PLANE - 1)
            to = (pl.ds(t * order, order), pl.ds(a * LANES + (b % 2) * 64, 64))
            yhigh_ref[to] = rhigh_ref[plane, t - first, n][:, half]
            ylow_ref[to] = rlow_ref[plane, t - first, n][:, half]


def block_diagonal(v, low_lane, real_lane):
    turned = times_i(v, real_lane)
    zero = jnp.zeros_like(v)
    return jnp.concatenate(
        [
            jnp.where(low_lane, v, zero),
            jnp.where(low_lane, turned, zero),
            jnp.where(low_lane, zero, v),
            jnp.where(low_lane, zero, turned),
        ],
        axis=0,
    )


def weights_of(v, low_lane, real_lane):
    high, low = split(block_diagonal(v, low_lane, real_lane))
    return jnp.concatenate([high, low], axis=1)


def pair_product(u, weights, order):
    high, low = split(u)
    o = dot(jnp.concatenate([high, low], axis=0), weights)
    return o[:order, :LANES] + o[order:, :LANES] + o[:order, LANES:]


def path_and_project(own, g2_ref, yhigh_ref, ylow_ref, wt_ref, gaunt_ref, v_ref, order):
    low_lane, real_lane = tile_masks(order)
    low2, _ = tile_masks(2 * order)
    both = g2_ref[...]
    rows = both.shape[0] // 2
    half = rows // 2
    gh = both[:rows]
    pairs = range(PLANE // 2)
    cs = []
    for pair in pairs:
        lanes = pl.ds(pair * 2 * LANES, 2 * LANES)
        d = dot(both, yhigh_ref[:, lanes])
        s = d[:rows] + d[rows:] + dot(gh, ylow_ref[:, lanes])
        e0, o0 = s[:half, :LANES], s[half:, :LANES]
        e1, o1 = s[:half, LANES:], s[half:, LANES:]
        m = jnp.where(low2, e0, o1) + pltpu.roll(jnp.where(low2, e1, o0), 64, 1)
        cs.append(m[:order] + times_i(m[order:], real_lane))
    qs = [pair_product(cs[pair], wt_ref[pair], order) for pair in pairs]
    ws = [weights_of(q, low_lane, real_lane) for q in qs]
    ts = [own(pair) for pair in pairs]
    vs = ts
    for _ in range(TERMS - 1):
        vs = [ts[pair] + pair_product(vs[pair], ws[pair], order) for pair in pairs]
    for pair in pairs:
        v_ref[pl.ds(pair * order, order), :] = vs[pair]
    pairs = PLANE // 2
    lane = lax.broadcasted_iota(jnp.int32, (pairs, LANES), 1) // 32
    columns = []
    for block in range(order // 4):
        us = [v_ref[pl.ds(4 * block + ii, pairs, stride=order), :] for ii in range(4)]
        pieces = []
        for part in range(4):
            z = us[0] if part == 0 else pltpu.roll(us[0], (-part * 32) % LANES, 1)
            for ii in range(1, 4):
                shift = ((ii - part) * 32) % LANES
                z = jnp.where(lane == ii, us[ii] if shift == 0 else pltpu.roll(us[ii], shift, 1), z)
            pieces.append(z)
        columns.append(jnp.concatenate(pieces, axis=0))
    z = jnp.concatenate(columns, axis=1)
    zh, zl = split(z)
    gh, gl = gaunt_ref[0], gaunt_ref[1]
    nt = (((1,), (1,)), ((), ()))
    d = lax.dot_general(jnp.concatenate([zh, zl], axis=0), gh, nt, preferred_element_type=f32)
    return d[: 2 * PLANE] + d[2 * PLANE :] + lax.dot_general(zh, gl, nt, preferred_element_type=f32)


def store_scaled(projected, wr, wi, coef_ref):
    pairs = PLANE // 2
    for a2 in range(2):
        re = projected[a2 * 2 * pairs : a2 * 2 * pairs + pairs]
        im = projected[a2 * 2 * pairs + pairs : (a2 + 1) * 2 * pairs]
        coef_ref[0, pl.ds(a2, pairs, stride=2), :] = wr * re - wi * im
        coef_ref[1, pl.ds(a2, pairs, stride=2), :] = wr * im + wi * re


def ends_of(dirs):
    return ((0, 9), (9, 17), (17, dirs))


def plan(dirs):
    ends = ends_of(dirs)
    firsts = tuple((dirs - stop) // 2 for _, stop in ends)
    counts = tuple((dirs - 1 - start) // 2 - first + 1 for (start, _), first in zip(ends, firsts))
    return firsts, counts


def density_of(kind, coef_ref, pieces_ref, density_ref):
    energies, kinds = pieces_ref.shape[:2]
    channels, atoms, width = density_ref.shape
    kind = jnp.broadcast_to(kind, (atoms, width))
    for l in range(channels):
        total = None
        for e in range(energies):
            for z in range(2):
                row = jnp.broadcast_to(pieces_ref[e, 0, l, 1 - z : 2 - z, :], (atoms, width))
                for s in range(1, kinds):
                    row = jnp.where(kind == s, pieces_ref[e, s, l, 1 - z : 2 - z, :], row)
                term = coef_ref[e, z, :, l : l + 1] * row
                total = term if total is None else total + term
        density_ref[l] = total


def core(order, dirs, ring, energies, nbr_ref, w_ref, valence_ref, own_ref, g_ref, gaunt_ref, shapes_ref,
         weights_ref, species_ref, madelung_ref, density_ref, shift_ref,
         coef_ref, pieces_ref, total_ref, wd_ref, table_ref, halo_ref, q_ref, mine_ref, wg_ref, wt_ref, rhs_ref, g2_ref, lhs_ref, rhigh_ref, rlow_ref,
         yhigh_ref, ylow_ref, v_ref, halo_send, halo_recv, piece_send, piece_recv, coef_send, coef_recv,
         q_send, q_recv, local_sem):
    atom, energy = lax.axis_index("atom"), lax.axis_index("energy")
    devices = ring * energies
    me = atom * energies + energy
    kinds, width = shapes_ref.shape[0], pieces_ref.shape[4]

    def place(step):
        other = lax.rem(me + step, devices)
        return {"atom": other // energies, "energy": lax.rem(other, energies)}

    barrier = pltpu.get_barrier_semaphore()

    def greet(step, carry):
        pl.semaphore_signal(barrier, inc=1, device_id=place(step), device_id_type=MESH)
        return carry

    lax.fori_loop(1, devices, greet, 0)

    firsts, counts = plan(dirs)
    to_rows(lambda m, lanes: g_ref[:, m // 2, m % 2, lanes], dirs // 2, wg_ref, order)
    prepare_couplings(wg_ref, rhs_ref, g2_ref, order, dirs // 2)
    pl.semaphore_wait(barrier, devices - 1)

    right, left = lax.rem(atom + 1, ring), lax.rem(atom + ring - 1, ring)
    halos = []
    for side, target in ((0, right), (1, left)):
        copy = pltpu.make_async_remote_copy(
            src_ref=own_ref, dst_ref=halo_ref.at[side], send_sem=halo_send.at[side],
            recv_sem=halo_recv.at[side], device_id={"atom": target, "energy": energy}, device_id_type=MESH,
        )
        copy.start()
        halos.append(copy)

    def slice_of(e):
        return shapes_ref.at[:, :, :, pl.ds(pl.multiple_of(e * width, LANES), width)]

    pieces = []
    for step in range(1, energies):
        other = lax.rem(energy + step, energies)
        copy = pltpu.make_async_remote_copy(
            src_ref=slice_of(other), dst_ref=pieces_ref.at[energy], send_sem=piece_send.at[step],
            recv_sem=piece_recv.at[step], device_id={"atom": atom, "energy": other}, device_id_type=MESH,
        )
        copy.start()
        pieces.append(copy)
    keep = pltpu.make_async_copy(slice_of(energy), pieces_ref.at[energy], local_sem)
    keep.start()

    def plane(index, raw):
        w = wt_ref.at[index]
        to_rows(raw, PLANE // 2, w, order)
        plane_products(lambda pair: tile_of(w, pair, order), lhs_ref, rhs_ref, rhigh_ref, rlow_ref,
                       index, firsts[index], counts[index], order)
        gather(nbr_ref, rhigh_ref, rlow_ref, yhigh_ref, ylow_ref, dirs, index, firsts[index], order)

    plane(1, lambda m, lanes: own_ref[:, m // 2, m % 2, lanes])

    low_lane, real_lane = tile_masks(order)
    for pair in range(PLANE // 2):
        wd_ref[pair] = weights_of(tile_of(wt_ref.at[1], pair, order), low_lane, real_lane)
    table_ref[0], table_ref[1] = split(gaunt_ref[...])

    row = lax.broadcasted_iota(jnp.int32, (PLANE, PLANE), 0)
    lane = lax.broadcasted_iota(jnp.int32, (PLANE, PLANE), 1)
    kinds_row = jnp.broadcast_to(species_ref[...].astype(f32), (PLANE, PLANE))
    kind = jnp.sum(jnp.where(row == lane, kinds_row, jnp.zeros((PLANE, PLANE), f32)), axis=1, keepdims=True)
    sums = [None, None]
    base = jnp.zeros(kind.shape, f32)
    for s in range(kinds):
        total = jnp.sum(shapes_ref[s, 0] * weights_ref[...], axis=1, keepdims=True)
        for z in range(2):
            value = jnp.broadcast_to(total[1 - z : 2 - z], kind.shape)
            sums[z] = value if s == 0 else jnp.where(kind == s, value, sums[z])
        base = jnp.where(kind == s, valence_ref[s], base)
    base = jnp.where(energy == 0, base, jnp.zeros_like(base))

    for side, index in ((0, 0), (1, 2)):
        halos[side].wait_recv()
        plane(index, lambda m, lanes, side=side: halo_ref[side, :, m // 2, m % 2, lanes])

    own = lambda pair: tile_of(wt_ref.at[1], pair, order)
    projected = path_and_project(own, g2_ref, yhigh_ref, ylow_ref, wd_ref, table_ref, v_ref, order)
    store_scaled(projected, w_ref[0, 0], w_ref[0, 1], mine_ref)

    q = mine_ref[0, :, 0:1] * sums[0] + mine_ref[1, :, 0:1] * sums[1] - base
    row = lax.broadcasted_iota(jnp.int32, (PLANE, LANES), 0)
    lane = lax.broadcasted_iota(jnp.int32, (PLANE, LANES), 1)
    spot = lane == row + PLANE * lax.rem(atom, LANES // PLANE)
    q_ref[me] = jnp.sum(jnp.where(spot, q, jnp.zeros((PLANE, LANES), f32)), axis=0, keepdims=True)

    def spread(step, carry):
        pltpu.make_async_remote_copy(
            src_ref=q_ref.at[me], dst_ref=q_ref.at[me], send_sem=q_send, recv_sem=q_recv,
            device_id=place(step), device_id_type=MESH,
        ).start()
        return carry

    lax.fori_loop(1, devices, spread, 0)
    coefs = []
    for step in range(1, energies):
        other = lax.rem(energy + step, energies)
        copy = pltpu.make_async_remote_copy(
            src_ref=mine_ref, dst_ref=coef_ref.at[energy], send_sem=coef_send.at[step],
            recv_sem=coef_recv.at[step], device_id={"atom": atom, "energy": other}, device_id_type=MESH,
        )
        copy.start()
        coefs.append(copy)
    coef_ref[energy] = mine_ref[...]

    keep.wait()
    for copy in pieces + coefs:
        copy.wait()
    density_of(kind, coef_ref, pieces_ref, total_ref)
    out = pltpu.make_async_copy(total_ref, density_ref, local_sem)
    out.start()
    for copy in halos:
        copy.wait_send()
    rest = q_ref.at[pl.ds(0, devices - 1)]
    pltpu.make_async_copy(rest, rest, q_send).wait()
    pltpu.make_async_copy(rest, rest, q_recv).wait()
    group = LANES // PLANE * energies
    shift = jnp.zeros((PLANE, 1), f32)
    for g in range(ring * PLANE // LANES):
        charges = jnp.sum(q_ref[pl.ds(g * group, group), 0, :], axis=0, keepdims=True)
        shift = shift + jnp.sum(madelung_ref[:, pl.ds(g * LANES, LANES)] * charges, axis=1, keepdims=True)
    shift_ref[...] = shift
    out.wait()


def core_scratch(order, dirs, ring, energies, channels, kinds, width):
    count = max(plan(dirs)[1])
    depth = dirs // 2 * order
    dma = pltpu.SemaphoreType.DMA
    return [
        pltpu.VMEM((energies, 2, PLANE, channels), f32),
        pltpu.VMEM((energies, kinds, channels, 2, width), f32),
        pltpu.VMEM((channels, PLANE, width), f32),
        pltpu.VMEM((PLANE // 2, LANES, 2 * LANES), bf16),
        pltpu.VMEM((2, channels, order * order), bf16),
        pltpu.VMEM((2, PLANE // 2, 2, 2, order * order), f32),
        pltpu.VMEM((ring * energies, 1, LANES), f32),
        pltpu.VMEM((2, PLANE, channels), f32),
        pltpu.VMEM((order * 16, LANES), f32),
        pltpu.VMEM((3, order * (PLANE // 2), LANES), f32),
        pltpu.VMEM((8 * order, dirs * 64), bf16),
        pltpu.VMEM((8 * order, depth), bf16),
        pltpu.VMEM((PLANE * order, LANES), bf16),
        pltpu.VMEM((3, count, PLANE, order, LANES), bf16),
        pltpu.VMEM((3, count, PLANE, order, LANES), bf16),
        pltpu.VMEM((depth, PLANE * LANES), bf16),
        pltpu.VMEM((depth, PLANE * LANES), bf16),
        pltpu.VMEM((PLANE // 2 * order, LANES), f32),
        dma((2,)), dma((2,)), dma((energies,)), dma((energies,)), dma((energies,)), dma((energies,)),
        dma, dma, dma,
    ]


VMEM = pl.BlockSpec(memory_space=pltpu.VMEM)
SMEM = pl.BlockSpec(memory_space=pltpu.SMEM)
MESH = pl.DeviceIdType.MESH


def shards(single_site, structure, neighbours, species, valence, energy_weights, gaunt_table,
           radial_shapes, radial_weights, madelung, old_potential):
    atom_rows, energy_rows = single_site.shape[:2]
    dirs = structure.shape[1]
    order = int(round(single_site.shape[3] ** 0.5))
    channels, width = old_potential.shape[1], old_potential.shape[2]
    kinds = radial_shapes.shape[0]
    energies = lax.axis_size("energy")
    assert atom_rows == PLANE and energy_rows == 1 and order == 32

    def parts(x):
        return x.reshape(-1, 2, 2, order * order)

    shapes = jnp.transpose(radial_shapes[:, 0], (0, 2, 1, 3))
    ring = lax.axis_size("atom")
    density, shift = pl.pallas_call(
        functools.partial(core, order, dirs, ring, energies),
        out_shape=[
            jax.ShapeDtypeStruct((channels, atom_rows, width), f32),
            jax.ShapeDtypeStruct((atom_rows, 1), f32),
        ],
        in_specs=[SMEM] * 3 + [VMEM] * 7,
        out_specs=[pl.BlockSpec(memory_space=pl.ANY), VMEM],
        scratch_shapes=core_scratch(order, dirs, ring, energies, channels, kinds, width),
        compiler_params=pltpu.CompilerParams(collective_id=0, has_side_effects=True),
        name="scatter",
    )(neighbours, energy_weights, valence, parts(single_site), parts(structure), gaunt_table, shapes,
      radial_weights[None, :], species[None, :], madelung)

    old = jnp.transpose(old_potential, (1, 0, 2))
    channel = lax.broadcasted_iota(jnp.int32, (channels, 1, 1), 0)
    added = jnp.where(channel == 0, shift[None], jnp.float32(0.0))
    potential = (1.0 - mixing) * old + mixing * (density + added)
    back = lambda x: jnp.transpose(x, (1, 0, 2))
    return back(density), back(potential)


def solution(mesh):
    in_specs = (
        P("atom", "energy", None, None),
        P("energy", None, None, None),
        P("atom", None),
        P("atom"),
        P(),
        P("energy", None),
        P(),
        P(None, "energy", None, None, None),
        P(),
        P("atom", None),
        P("atom", None, "energy"),
    )
    out_specs = (P("atom", None, "energy"), P("atom", None, "energy"))
    return jax.shard_map(shards, mesh=mesh, in_specs=in_specs, out_specs=out_specs, check_vma=False)
```

```python
import functools

import jax
import jax.numpy as jnp
from jax import lax
from jax.experimental import pallas as pl
from jax.experimental.pallas import tpu as pltpu
from jax.sharding import PartitionSpec as P

PLANE = 16
TERMS = 4
LANES = 128

mixing = 0.3
f32 = jnp.float32
bf16 = jnp.bfloat16


def split(x):
    high = x.astype(bf16)
    return high, (x - high.astype(f32)).astype(bf16)


def tile_masks(rows):
    lane = lax.broadcasted_iota(jnp.int32, (rows, LANES), 1)
    return lane < 64, (lane & 32) == 0


def times_i(x, real_lane):
    return jnp.where(real_lane, -pltpu.roll(x, 96, 1), pltpu.roll(x, 32, 1))


def dot(a, b):
    return jnp.dot(a, b, preferred_element_type=f32)


def to_rows(raw, tiles, w_ref, order):
    stride = w_ref.shape[0] // order
    lane = lax.broadcasted_iota(jnp.int32, (tiles, LANES), 1) // 32
    for block in range(order // 4):
        parts = [raw(m, pl.ds(block * LANES, LANES)) for m in range(4)]
        for ii in range(4):
            u = None
            for m in range(4):
                shift = ((m - ii) * 32) % LANES
                x = parts[m] if shift == 0 else pltpu.roll(parts[m], shift, 1)
                u = x if u is None else jnp.where(lane == m, x, u)
            w_ref[pl.ds((4 * block + ii) * stride, tiles), :] = u


def tile_of(w_ref, tile, order):
    return w_ref[pl.ds(tile, order, stride=w_ref.shape[0] // order), :]


def prepare_couplings(w_ref, rhs_ref, g2_ref, order, blocks):
    _, real_lane = tile_masks(order)
    lane = lax.broadcasted_iota(jnp.int32, (order, LANES), 1) // 32
    joined = [None] * 4
    for t in range(blocks):
        g = tile_of(w_ref, t, order)
        high, low = split(jnp.concatenate([g, times_i(g, real_lane)], axis=0))
        rhs_ref[:, pl.ds(t * LANES, LANES)] = jnp.concatenate([high, high, low, low], axis=0)
    for t in range(blocks):
        g = tile_of(w_ref, blocks - 1 - t, order)
        place = t % 4
        for parity in range(2):
            for z in range(2):
                row = parity * 2 + z
                chunk = (2 - 2 * parity + z) % 4
                shift = ((place - chunk) * 32) % LANES
                x = g if shift == 0 else pltpu.roll(g, shift, 1)
                joined[row] = x if place == 0 else jnp.where(lane == place, x, joined[row])
                if place == 3 or t == blocks - 1:
                    lanes = pl.ds(t // 4 * LANES, 32 * (place + 1))
                    high, low = split(joined[row][:, : 32 * (place + 1)])
                    g2_ref[pl.ds(row * order, order), lanes] = high
                    g2_ref[pl.ds((4 + row) * order, order), lanes] = low


def plane_products(x, lhs_ref, rhs_ref, rhigh_ref, rlow_ref, plane, first, count, order):
    low_lane, _ = tile_masks(order)
    for pair in range(PLANE // 2):
        v = x(pair)
        high = v.astype(bf16).astype(f32)
        low = v - high
        even = jnp.where(low_lane, high, pltpu.roll(low, 64, 1))
        odd = jnp.where(low_lane, pltpu.roll(high, 64, 1), low)
        lhs_ref[pl.ds(pair * 2 * order, 2 * order), :] = jnp.concatenate(
            [even, odd], axis=0
        ).astype(bf16)
    lhs = lhs_ref[...]
    lhs = jnp.concatenate([lhs, lhs], axis=1)
    for t in range(count):
        r = dot(lhs, rhs_ref[:, pl.ds((first + t) * LANES, LANES)])
        high, low = split(r)
        rhigh_ref[plane, t] = high.reshape(PLANE, order, LANES)
        rlow_ref[plane, t] = low.reshape(PLANE, order, LANES)


def gather(nbr_ref, rhigh_ref, rlow_ref, yhigh_ref, ylow_ref, dirs, plane, first, order):
    start, stop = ends_of(dirs)[plane]
    for k in range(start, stop):
        b = dirs - 1 - k
        t = b // 2
        half = slice((b % 2) * 64, (b % 2) * 64 + 64)
        for a in range(PLANE):
            n = nbr_ref[a, k] & (PLANE - 1)
            to = (pl.ds(t * order, order), pl.ds(a * LANES + (b % 2) * 64, 64))
            yhigh_ref[to] = rhigh_ref[plane, t - first, n][:, half]
            ylow_ref[to] = rlow_ref[plane, t - first, n][:, half]


def block_diagonal(v, low_lane, real_lane):
    turned = times_i(v, real_lane)
    zero = jnp.zeros_like(v)
    return jnp.concatenate(
        [
            jnp.where(low_lane, v, zero),
            jnp.where(low_lane, turned, zero),
            jnp.where(low_lane, zero, v),
            jnp.where(low_lane, zero, turned),
        ],
        axis=0,
    )


def weights_of(v, low_lane, real_lane):
    high, low = split(block_diagonal(v, low_lane, real_lane))
    return jnp.concatenate([high, low], axis=1)


def pair_product(u, weights, order):
    high, low = split(u)
    o = dot(jnp.concatenate([high, low], axis=0), weights)
    return o[:order, :LANES] + o[order:, :LANES] + o[:order, LANES:]


def path_and_project(own, g2_ref, yhigh_ref, ylow_ref, wt_ref, gaunt_ref, v_ref, order):
    low_lane, real_lane = tile_masks(order)
    low2, _ = tile_masks(2 * order)
    both = g2_ref[...]
    rows = both.shape[0] // 2
    half = rows // 2
    gh = both[:rows]
    pairs = range(PLANE // 2)
    cs = []
    for pair in pairs:
        lanes = pl.ds(pair * 2 * LANES, 2 * LANES)
        d = dot(both, yhigh_ref[:, lanes])
        s = d[:rows] + d[rows:] + dot(gh, ylow_ref[:, lanes])
        e0, o0 = s[:half, :LANES], s[half:, :LANES]
        e1, o1 = s[:half, LANES:], s[half:, LANES:]
        m = jnp.where(low2, e0, o1) + pltpu.roll(jnp.where(low2, e1, o0), 64, 1)
        cs.append(m[:order] + times_i(m[order:], real_lane))
    qs = [pair_product(cs[pair], wt_ref[pair], order) for pair in pairs]
    ws = [weights_of(q, low_lane, real_lane) for q in qs]
    ts = [own(pair) for pair in pairs]
    vs = ts
    for _ in range(TERMS - 1):
        vs = [ts[pair] + pair_product(vs[pair], ws[pair], order) for pair in pairs]
    for pair in pairs:
        v_ref[pl.ds(pair * order, order), :] = vs[pair]
    pairs = PLANE // 2
    lane = lax.broadcasted_iota(jnp.int32, (pairs, LANES), 1) // 32
    columns = []
    for block in range(order // 4):
        us = [v_ref[pl.ds(4 * block + ii, pairs, stride=order), :] for ii in range(4)]
        pieces = []
        for part in range(4):
            z = us[0] if part == 0 else pltpu.roll(us[0], (-part * 32) % LANES, 1)
            for ii in range(1, 4):
                shift = ((ii - part) * 32) % LANES
                z = jnp.where(lane == ii, us[ii] if shift == 0 else pltpu.roll(us[ii], shift, 1), z)
            pieces.append(z)
        columns.append(jnp.concatenate(pieces, axis=0))
    z = jnp.concatenate(columns, axis=1)
    zh, zl = split(z)
    gh, gl = gaunt_ref[0], gaunt_ref[1]
    nt = (((1,), (1,)), ((), ()))
    d = lax.dot_general(jnp.concatenate([zh, zl], axis=0), gh, nt, preferred_element_type=f32)
    return d[: 2 * PLANE] + d[2 * PLANE :] + lax.dot_general(zh, gl, nt, preferred_element_type=f32)


def store_scaled(projected, wr, wi, coef_ref):
    pairs = PLANE // 2
    for a2 in range(2):
        re = projected[a2 * 2 * pairs : a2 * 2 * pairs + pairs]
        im = projected[a2 * 2 * pairs + pairs : (a2 + 1) * 2 * pairs]
        coef_ref[0, pl.ds(a2, pairs, stride=2), :] = wr * re - wi * im
        coef_ref[1, pl.ds(a2, pairs, stride=2), :] = wr * im + wi * re


def ends_of(dirs):
    return ((0, 9), (9, 17), (17, dirs))


def plan(dirs):
    ends = ends_of(dirs)
    firsts = tuple((dirs - stop) // 2 for _, stop in ends)
    counts = tuple((dirs - 1 - start) // 2 - first + 1 for (start, _), first in zip(ends, firsts))
    return firsts, counts


def density_of(kind, coef_ref, pieces_ref, old_ref, density_ref, mixed_ref):
    energies, kinds = pieces_ref.shape[:2]
    channels, atoms, width = density_ref.shape
    kind = jnp.broadcast_to(kind, (atoms, width))
    for l in range(channels):
        total = None
        for e in range(energies):
            for z in range(2):
                row = jnp.broadcast_to(pieces_ref[e, 0, l, 1 - z : 2 - z, :], (atoms, width))
                for s in range(1, kinds):
                    row = jnp.where(kind == s, pieces_ref[e, s, l, 1 - z : 2 - z, :], row)
                term = coef_ref[e, z, :, l : l + 1] * row
                total = term if total is None else total + term
        density_ref[l] = total
        if l > 0:
            mixed_ref[l - 1] = (1.0 - mixing) * old_ref[l] + mixing * total


def core(order, dirs, ring, energies, nbr_ref, w_ref, valence_ref, own_ref, g_ref, gaunt_ref, shapes_ref,
         weights_ref, species_ref, madelung_ref, previous_ref, density_ref, potential_ref,
         coef_ref, pieces_ref, total_ref, old_ref, mixed_ref, first_ref, wd_ref, table_ref, halo_ref, q_ref, mine_ref, wg_ref, wt_ref, rhs_ref, g2_ref, lhs_ref, rhigh_ref, rlow_ref,
         yhigh_ref, ylow_ref, v_ref, halo_send, halo_recv, piece_send, piece_recv, coef_send, coef_recv,
         q_send, q_recv, local_sem, old_sem, mixed_sem, first_sem):
    atom, energy = lax.axis_index("atom"), lax.axis_index("energy")
    devices = ring * energies
    me = atom * energies + energy
    kinds, width = shapes_ref.shape[0], pieces_ref.shape[4]

    def place(step):
        other = lax.rem(me + step, devices)
        return {"atom": other // energies, "energy": lax.rem(other, energies)}

    fetch = pltpu.make_async_copy(previous_ref, old_ref, old_sem)
    fetch.start()
    barrier = pltpu.get_barrier_semaphore()

    def greet(step, carry):
        pl.semaphore_signal(barrier, inc=1, device_id=place(step), device_id_type=MESH)
        return carry

    lax.fori_loop(1, devices, greet, 0)

    firsts, counts = plan(dirs)
    to_rows(lambda m, lanes: g_ref[:, m // 2, m % 2, lanes], dirs // 2, wg_ref, order)
    prepare_couplings(wg_ref, rhs_ref, g2_ref, order, dirs // 2)
    pl.semaphore_wait(barrier, devices - 1)

    right, left = lax.rem(atom + 1, ring), lax.rem(atom + ring - 1, ring)
    halos = []
    for side, target in ((0, right), (1, left)):
        copy = pltpu.make_async_remote_copy(
            src_ref=own_ref, dst_ref=halo_ref.at[side], send_sem=halo_send.at[side],
            recv_sem=halo_recv.at[side], device_id={"atom": target, "energy": energy}, device_id_type=MESH,
        )
        copy.start()
        halos.append(copy)

    def slice_of(e):
        return shapes_ref.at[:, :, :, pl.ds(pl.multiple_of(e * width, LANES), width)]

    pieces = []
    for step in range(1, energies):
        other = lax.rem(energy + step, energies)
        copy = pltpu.make_async_remote_copy(
            src_ref=slice_of(other), dst_ref=pieces_ref.at[energy], send_sem=piece_send.at[step],
            recv_sem=piece_recv.at[step], device_id={"atom": atom, "energy": other}, device_id_type=MESH,
        )
        copy.start()
        pieces.append(copy)
    keep = pltpu.make_async_copy(slice_of(energy), pieces_ref.at[energy], local_sem)
    keep.start()

    def plane(index, raw):
        w = wt_ref.at[index]
        to_rows(raw, PLANE // 2, w, order)
        plane_products(lambda pair: tile_of(w, pair, order), lhs_ref, rhs_ref, rhigh_ref, rlow_ref,
                       index, firsts[index], counts[index], order)
        gather(nbr_ref, rhigh_ref, rlow_ref, yhigh_ref, ylow_ref, dirs, index, firsts[index], order)

    plane(1, lambda m, lanes: own_ref[:, m // 2, m % 2, lanes])

    low_lane, real_lane = tile_masks(order)
    for pair in range(PLANE // 2):
        wd_ref[pair] = weights_of(tile_of(wt_ref.at[1], pair, order), low_lane, real_lane)
    table_ref[0], table_ref[1] = split(gaunt_ref[...])

    row = lax.broadcasted_iota(jnp.int32, (PLANE, PLANE), 0)
    lane = lax.broadcasted_iota(jnp.int32, (PLANE, PLANE), 1)
    kinds_row = jnp.broadcast_to(species_ref[...].astype(f32), (PLANE, PLANE))
    kind = jnp.sum(jnp.where(row == lane, kinds_row, jnp.zeros((PLANE, PLANE), f32)), axis=1, keepdims=True)
    sums = [None, None]
    base = jnp.zeros(kind.shape, f32)
    for s in range(kinds):
        total = jnp.sum(shapes_ref[s, 0] * weights_ref[...], axis=1, keepdims=True)
        for z in range(2):
            value = jnp.broadcast_to(total[1 - z : 2 - z], kind.shape)
            sums[z] = value if s == 0 else jnp.where(kind == s, value, sums[z])
        base = jnp.where(kind == s, valence_ref[s], base)
    base = jnp.where(energy == 0, base, jnp.zeros_like(base))

    for side, index in ((0, 0), (1, 2)):
        halos[side].wait_recv()
        plane(index, lambda m, lanes, side=side: halo_ref[side, :, m // 2, m % 2, lanes])

    own = lambda pair: tile_of(wt_ref.at[1], pair, order)
    projected = path_and_project(own, g2_ref, yhigh_ref, ylow_ref, wd_ref, table_ref, v_ref, order)
    store_scaled(projected, w_ref[0, 0], w_ref[0, 1], mine_ref)

    q = mine_ref[0, :, 0:1] * sums[0] + mine_ref[1, :, 0:1] * sums[1] - base
    row = lax.broadcasted_iota(jnp.int32, (PLANE, LANES), 0)
    lane = lax.broadcasted_iota(jnp.int32, (PLANE, LANES), 1)
    spot = lane == row + PLANE * lax.rem(atom, LANES // PLANE)
    q_ref[me] = jnp.sum(jnp.where(spot, q, jnp.zeros((PLANE, LANES), f32)), axis=0, keepdims=True)

    def spread(step, carry):
        pltpu.make_async_remote_copy(
            src_ref=q_ref.at[me], dst_ref=q_ref.at[me], send_sem=q_send, recv_sem=q_recv,
            device_id=place(step), device_id_type=MESH,
        ).start()
        return carry

    lax.fori_loop(1, devices, spread, 0)
    coefs = []
    for step in range(1, energies):
        other = lax.rem(energy + step, energies)
        copy = pltpu.make_async_remote_copy(
            src_ref=mine_ref, dst_ref=coef_ref.at[energy], send_sem=coef_send.at[step],
            recv_sem=coef_recv.at[step], device_id={"atom": atom, "energy": other}, device_id_type=MESH,
        )
        copy.start()
        coefs.append(copy)
    coef_ref[energy] = mine_ref[...]

    keep.wait()
    for copy in pieces + coefs:
        copy.wait()
    fetch.wait()
    density_of(kind, coef_ref, pieces_ref, old_ref, total_ref, mixed_ref)
    out = pltpu.make_async_copy(total_ref, density_ref, local_sem)
    out.start()
    upper = pltpu.make_async_copy(mixed_ref, potential_ref.at[pl.ds(1, mixed_ref.shape[0])], mixed_sem)
    upper.start()
    for copy in halos:
        copy.wait_send()
    rest = q_ref.at[pl.ds(0, devices - 1)]
    pltpu.make_async_copy(rest, rest, q_send).wait()
    pltpu.make_async_copy(rest, rest, q_recv).wait()
    group = LANES // PLANE * energies
    shift = jnp.zeros((PLANE, 1), f32)
    for g in range(ring * PLANE // LANES):
        charges = jnp.sum(q_ref[pl.ds(g * group, group), 0, :], axis=0, keepdims=True)
        shift = shift + jnp.sum(madelung_ref[:, pl.ds(g * LANES, LANES)] * charges, axis=1, keepdims=True)
    first_ref[0] = (1.0 - mixing) * old_ref[0] + mixing * (total_ref[0] + shift)
    last = pltpu.make_async_copy(first_ref, potential_ref.at[pl.ds(0, 1)], first_sem)
    last.start()
    out.wait()
    upper.wait()
    last.wait()


def core_scratch(order, dirs, ring, energies, channels, kinds, width):
    count = max(plan(dirs)[1])
    depth = dirs // 2 * order
    dma = pltpu.SemaphoreType.DMA
    return [
        pltpu.VMEM((energies, 2, PLANE, channels), f32),
        pltpu.VMEM((energies, kinds, channels, 2, width), f32),
        pltpu.VMEM((channels, PLANE, width), f32),
        pltpu.VMEM((channels, PLANE, width), f32),
        pltpu.VMEM((channels - 1, PLANE, width), f32),
        pltpu.VMEM((1, PLANE, width), f32),
        pltpu.VMEM((PLANE // 2, LANES, 2 * LANES), bf16),
        pltpu.VMEM((2, channels, order * order), bf16),
        pltpu.VMEM((2, PLANE // 2, 2, 2, order * order), f32),
        pltpu.VMEM((ring * energies, 1, LANES), f32),
        pltpu.VMEM((2, PLANE, channels), f32),
        pltpu.VMEM((order * 16, LANES), f32),
        pltpu.VMEM((3, order * (PLANE // 2), LANES), f32),
        pltpu.VMEM((8 * order, dirs * 64), bf16),
        pltpu.VMEM((8 * order, depth), bf16),
        pltpu.VMEM((PLANE * order, LANES), bf16),
        pltpu.VMEM((3, count, PLANE, order, LANES), bf16),
        pltpu.VMEM((3, count, PLANE, order, LANES), bf16),
        pltpu.VMEM((depth, PLANE * LANES), bf16),
        pltpu.VMEM((depth, PLANE * LANES), bf16),
        pltpu.VMEM((PLANE // 2 * order, LANES), f32),
        dma((2,)), dma((2,)), dma((energies,)), dma((energies,)), dma((energies,)), dma((energies,)),
        dma, dma, dma, dma, dma, dma,
    ]


VMEM = pl.BlockSpec(memory_space=pltpu.VMEM)
SMEM = pl.BlockSpec(memory_space=pltpu.SMEM)
ANY = pl.BlockSpec(memory_space=pl.ANY)
MESH = pl.DeviceIdType.MESH


def shards(single_site, structure, neighbours, species, valence, energy_weights, gaunt_table,
           radial_shapes, radial_weights, madelung, old_potential):
    atom_rows, energy_rows = single_site.shape[:2]
    dirs = structure.shape[1]
    order = int(round(single_site.shape[3] ** 0.5))
    channels, width = old_potential.shape[1], old_potential.shape[2]
    kinds = radial_shapes.shape[0]
    energies = lax.axis_size("energy")
    assert atom_rows == PLANE and energy_rows == 1 and order == 32

    def parts(x):
        return x.reshape(-1, 2, 2, order * order)

    shapes = jnp.transpose(radial_shapes[:, 0], (0, 2, 1, 3))
    ring = lax.axis_size("atom")
    density, potential = pl.pallas_call(
        functools.partial(core, order, dirs, ring, energies),
        out_shape=[jax.ShapeDtypeStruct((channels, atom_rows, width), f32)] * 2,
        in_specs=[SMEM] * 3 + [VMEM] * 7 + [ANY],
        out_specs=[ANY] * 2,
        scratch_shapes=core_scratch(order, dirs, ring, energies, channels, kinds, width),
        compiler_params=pltpu.CompilerParams(collective_id=0, has_side_effects=True),
        name="scatter",
    )(neighbours, energy_weights, valence, parts(single_site), parts(structure), gaunt_table, shapes,
      radial_weights[None, :], species[None, :], madelung,
      jnp.transpose(old_potential, (1, 0, 2)))

    back = lambda x: jnp.transpose(x, (1, 0, 2))
    return back(density), back(potential)


def solution(mesh):
    in_specs = (
        P("atom", "energy", None, None),
        P("energy", None, None, None),
        P("atom", None),
        P("atom"),
        P(),
        P("energy", None),
        P(),
        P(None, "energy", None, None, None),
        P(),
        P("atom", None),
        P("atom", None, "energy"),
    )
    out_specs = (P("atom", None, "energy"), P("atom", None, "energy"))
    return jax.shard_map(shards, mesh=mesh, in_specs=in_specs, out_specs=out_specs, check_vma=False)
```
